1024 devices in a mesh: fsdp: 64 (over z, y_lo), rep: 4 (over x), dp: 4 (over y_hi, core).
Axes of the slice: x: 4, y: 4 (y_hi: 2, y_lo: 2; y = y_hi * 2 + y_lo), z: 32, core: 2. Of those that a mesh axis runs over, the one named last changes fastest.
Arguments:
- trainer_gate: bfloat16 [8192, 4, 4096], P('fsdp', 'dp'), may hold values from -0.0625 to 0.0625
- trainer_up: bfloat16 [8192, 4, 4096], P('fsdp', 'dp'), may hold values from -0.0625 to 0.0625
- owner_map: int32 [64], replicated, may hold values from 0 to 63, each once
- sketch_seeds: int32 [8192], replicated, may hold values from 0 to 1
- probes: bfloat16 [4, 64, 128, 8192], P('rep', 'fsdp'), may hold values from -6 to 6
Outputs:
- digest: float32 [2, 64, 4, 4096], P(None, None, 'dp', 'fsdp')
- hidden: bfloat16 [4, 64, 128, 4, 256], P('rep', 'fsdp', None, 'dp')
The draws below stay inside these ranges and needn't reach their ends.
Inputs may be any that keep to these rules, and one draw needn't show every extreme that they name: owner_map is a permutation: every true row block is held at exactly one trainer position.
All inputs are finite; a program needn't handle non-finite values.
Results may differ from the reference program's by a relative error of at most 0.01.
Values may be sent and summed in bfloat16 or wider, within the bound.
No kernel may reach another device: no remote copies, remote signals or barrier semaphores. Data moves between devices by JAX's collectives and lax.ppermute only.
A program may use at most 64 MiB of HBM per device.

```python
import jax
import jax.numpy as jnp
from jax import lax

D = 8192
FDP = 4096
PROBE = 128
BLOCKS = 64
N_FSDP = 64
N_REP = 4
N_DP = 4


def with_ends(array, key, low, high):
    shape = array.shape
    place = [jax.random.randint(jax.random.fold_in(key, axis), (), 0, shape[axis]) for axis in range(len(shape))]
    array = array.at[tuple(place)].set(low)
    longest = shape.index(max(shape))
    place[longest] = (place[longest] + 1) % shape[longest]
    return array.at[tuple(place)].set(high)


def steps_of(rng, extent, cuts, low, high):
    loudness, own = 1.0, jax.random.fold_in(rng, 6)
    for position, blocks in cuts:
        steps = jnp.exp(jax.random.uniform(jax.random.fold_in(own, position), (blocks,), jnp.float32, low / len(cuts), high / len(cuts)))
        loudness = loudness * jnp.repeat(steps, extent[position] // blocks).reshape([-1 if axis == position else 1 for axis in range(len(extent))])
    return loudness


def bell_draw(rng, dims, scale, reach, cuts=(), held_as=jnp.bfloat16):
    drawn = jax.random.normal(rng, dims, jnp.float32) * scale
    if len(cuts) > 0:
        drawn = steps_of(rng, dims, cuts, -0.22, 0.18) * drawn
    return jnp.clip(drawn, min=-reach, max=reach).astype(held_as)


def setup_inputs(seed: int = 0) -> dict:
    keys = jax.random.split(jax.random.key(seed), 6)
    return {
        "trainer_gate": bell_draw(keys[0], (D, N_DP, FDP), D ** -0.5, 0.0625, ((0, 64), (1, 4))),
        "trainer_up": bell_draw(keys[1], (D, N_DP, FDP), D ** -0.5, 0.0625, ((0, 64), (1, 4))),
        "owner_map": jax.random.permutation(keys[2], BLOCKS).astype(jnp.int32),
        "sketch_seeds": with_ends(jax.random.randint(keys[3], (D,), 0, 2), jax.random.fold_in(keys[3], 1), 0, 1).astype(jnp.int32),
        "probes": bell_draw(keys[4], (N_REP, N_FSDP, PROBE, D), 1.0, 6.0, ((0, 4), (1, 64))),
    }


def restore(matrix, inverse):
    blocks_all = D // 128
    pieces = matrix.reshape(blocks_all, 128 * N_DP * FDP)
    return pieces[inverse].reshape(D, N_DP, FDP)

def sketch(matrix, signs):
    blocks_all = D // 128
    viewed = matrix.reshape(blocks_all, 128, N_DP, FDP).astype(jnp.float32)
    return 8.0 * lax.optimization_barrier(jnp.sum(signs * viewed, axis=1))

def reference(trainer_gate, trainer_up, owner_map, sketch_seeds, probes):
    ranks = min(16, N_FSDP)
    subs = N_FSDP // ranks
    width = FDP // ranks
    inverse = jnp.argsort(owner_map).astype(jnp.int32)
    gate_true = restore(trainer_gate, inverse)
    up_true = restore(trainer_up, inverse)
    signs = (1 - 2 * sketch_seeds).astype(jnp.float32).reshape(D // 128, 128, 1, 1)
    digest = jnp.stack([sketch(gate_true, signs), sketch(up_true, signs)])

    def one_device(member):
        rows = lax.dynamic_index_in_dim(probes, member, 1, keepdims=False)
        wide = rows.reshape(N_REP * PROBE, D).astype(jnp.float32)
        meansq = lax.optimization_barrier(jnp.mean(wide * wide, axis=-1, keepdims=True))
        normed = (wide / jnp.sqrt(meansq + 1e-05)).astype(jnp.bfloat16)
        start = member // subs * width
        gate_cols = lax.dynamic_slice_in_dim(gate_true, start, width, 2).reshape(D, N_DP * width)
        up_cols = lax.dynamic_slice_in_dim(up_true, start, width, 2).reshape(D, N_DP * width)
        gate_out = jnp.dot(normed, gate_cols, preferred_element_type=jnp.float32)
        up_out = jnp.dot(normed, up_cols, preferred_element_type=jnp.float32)
        result = (jax.nn.silu(gate_out) * up_out).astype(jnp.bfloat16)
        return result.reshape(N_REP, PROBE, N_DP, width)
    stacked = lax.map(one_device, jnp.arange(N_FSDP, dtype=jnp.int32))
    return (digest, jnp.transpose(stacked, (1, 0, 2, 3, 4)))
```

```python
import jax
import jax.numpy as jnp
import numpy as np
from jax import lax
from jax.sharding import Mesh, PartitionSpec as P

FSDP = ("ft", "fs")


def on_device(trainer_gate, trainer_up, owner_map, sketch_seeds, probes):
    rows, _, width = trainer_gate.shape
    n_rep = lax.axis_size("rep")
    n_ft = lax.axis_size("ft")
    n_fs = lax.axis_size("fs")
    n_f = n_ft * n_fs
    total_rows = rows * n_f
    blocks_all = total_rows // 128
    rank_width = width // n_ft
    narrow = rank_width // n_fs
    quarter = 128 // n_rep
    piece = quarter // n_fs
    replica = lax.axis_index("rep")
    member = lax.axis_index("ft") * n_fs + lax.axis_index("fs")
    sub = lax.axis_index("fs")

    weights = jnp.stack([trainer_gate.reshape(rows, width), trainer_up.reshape(rows, width)])

    mine = lax.dynamic_slice_in_dim(weights, replica * quarter, quarter, 1)
    send = mine.reshape(2, n_fs, piece, n_ft, rank_width).transpose(3, 1, 2, 0, 4)
    send = send.reshape(n_f, piece, 2 * rank_width)
    recv = lax.all_to_all(send, FSDP, 0, 0, tiled=True)

    positions = jnp.arange(blocks_all, dtype=jnp.int32)
    true_block = owner_map[member]
    signs = (1 - 2 * sketch_seeds).astype(jnp.float32)
    own_signs = lax.dynamic_slice_in_dim(signs, true_block * 128, 128, 0)
    digest_row = 8.0 * jnp.einsum(
        "k,pkc->pc", own_signs.astype(jnp.bfloat16), weights, preferred_element_type=jnp.float32
    )
    digest_send = digest_row.reshape(2, n_f, narrow).transpose(1, 0, 2)
    digest_recv = lax.all_to_all(digest_send, FSDP, 0, 0, tiled=True)

    inverse = jnp.sum(
        jnp.where(owner_map[None, :] == positions[:, None], positions[None, :], 0), axis=1
    )
    digest = digest_recv[inverse].transpose(1, 0, 2).reshape(2, blocks_all, 1, narrow)

    probe_rows = probes.shape[2]
    wide = probes.reshape(probe_rows, total_rows).astype(jnp.float32)
    meansq = jnp.mean(wide * wide, axis=-1, keepdims=True)
    normed = (wide / jnp.sqrt(meansq + 1e-05)).astype(jnp.bfloat16)
    normed_send = normed.reshape(probe_rows, blocks_all, n_rep, quarter).transpose(2, 0, 1, 3)
    normed_send = normed_send.reshape(n_rep, probe_rows, blocks_all * quarter)
    normed_recv = lax.all_to_all(normed_send, "rep", 0, 0, tiled=True)

    gathered = lax.all_gather(recv, "fs", axis=0, tiled=False)
    ordered = jnp.take(gathered, inverse, axis=1).transpose(1, 0, 2, 3)
    ordered = ordered.reshape(blocks_all * quarter, 2 * rank_width)

    lhs = normed_recv.reshape(n_rep * probe_rows, blocks_all * quarter)
    partial = jnp.dot(lhs, ordered, preferred_element_type=jnp.float32)
    partial = partial.reshape(n_rep, probe_rows, 2 * rank_width)
    summed = lax.psum_scatter(partial, "rep", scatter_dimension=0, tiled=True)
    gate_out = summed[0, :, :rank_width]
    up_out = summed[0, :, rank_width:]
    hidden = (jax.nn.silu(gate_out) * up_out).astype(jnp.bfloat16)
    return (digest, hidden.reshape(1, 1, probe_rows, 1, rank_width))


def solution(mesh):
    n_fsdp = mesh.shape["fsdp"]
    n_ft = min(16, n_fsdp)
    devices = np.asarray(mesh.devices).reshape(
        n_ft, n_fsdp // n_ft, mesh.shape["rep"], mesh.shape["dp"]
    )
    split = Mesh(devices, ("ft", "fs", "rep", "dp"))
    placed = (P(FSDP, "dp", None), P(FSDP, "dp", None), P(), P(), P("rep", FSDP, None, None))
    return jax.shard_map(
        on_device,
        mesh=split,
        in_specs=placed,
        out_specs=(P(None, None, "dp", FSDP), P("rep", FSDP, None, "dp", None)),
        check_vma=False,
    )
```

```python
import jax
import jax.numpy as jnp
import numpy as np
from jax import lax
from jax.sharding import Mesh, PartitionSpec as P

FSDP = ("ft", "fs")


def on_device(trainer_gate, trainer_up, owner_map, sketch_seeds, probes):
    rows, _, width = trainer_gate.shape
    n_rep = lax.axis_size("rep")
    n_ft = lax.axis_size("ft")
    n_fs = lax.axis_size("fs")
    n_f = n_ft * n_fs
    total_rows = rows * n_f
    blocks_all = total_rows // 128
    rank_width = width // n_ft
    narrow = rank_width // n_fs
    quarter = 128 // n_rep
    piece = quarter // n_fs
    replica = lax.axis_index("rep")
    member = lax.axis_index("ft") * n_fs + lax.axis_index("fs")
    sub = lax.axis_index("fs")

    weights = jnp.stack([trainer_gate.reshape(rows, width), trainer_up.reshape(rows, width)])

    mine = lax.dynamic_slice_in_dim(weights, replica * quarter, quarter, 1)
    send = mine.reshape(2, n_fs, piece, n_ft, rank_width).transpose(3, 1, 2, 0, 4)
    send = send.reshape(n_f, piece, 2 * rank_width)
    recv = lax.all_to_all(send, FSDP, 0, 0, tiled=True)

    positions = jnp.arange(blocks_all, dtype=jnp.int32)
    inverse = jnp.sum(
        jnp.where(owner_map[None, :] == positions[:, None], positions[None, :], 0), axis=1
    )

    probe_rows = probes.shape[2]
    wide = probes.reshape(probe_rows, total_rows).astype(jnp.float32)
    meansq = jnp.mean(wide * wide, axis=-1, keepdims=True)
    normed = (wide / jnp.sqrt(meansq + 1e-05)).astype(jnp.bfloat16)
    normed_send = normed.reshape(probe_rows, blocks_all, n_rep, quarter).transpose(2, 0, 1, 3)
    normed_send = normed_send.reshape(n_rep, probe_rows, blocks_all * quarter)
    normed_recv = lax.all_to_all(normed_send, "rep", 0, 0, tiled=True)

    signs = (1 - 2 * sketch_seeds).astype(jnp.float32).reshape(blocks_all, n_rep, quarter)
    own_signs = lax.dynamic_index_in_dim(signs, replica, 1, keepdims=False)
    sign_rows = jnp.eye(blocks_all, dtype=jnp.float32)[:, :, None] * own_signs[None, :, :]
    sign_rows = sign_rows.reshape(blocks_all, blocks_all * quarter).astype(jnp.bfloat16)

    gathered = lax.all_gather(recv, "fs", axis=0, tiled=False)
    ordered = jnp.take(gathered, inverse, axis=1).transpose(1, 0, 2, 3)
    ordered = ordered.reshape(blocks_all * quarter, 2 * rank_width)

    lhs = jnp.concatenate(
        [normed_recv.reshape(n_rep * probe_rows, blocks_all * quarter), sign_rows], axis=0
    )
    partial = jnp.dot(lhs, ordered, preferred_element_type=jnp.float32)
    hidden_part = partial[: n_rep * probe_rows].reshape(n_rep, probe_rows * 2 * rank_width)
    digest_part = partial[n_rep * probe_rows :].reshape(blocks_all, 2, n_fs, narrow)
    digest_part = lax.dynamic_index_in_dim(digest_part, sub, 2, keepdims=False)
    digest_part = jnp.broadcast_to(digest_part.reshape(1, -1), (n_rep, blocks_all * 2 * narrow))
    lanes = 128
    packed = jnp.concatenate([hidden_part, digest_part], axis=1).reshape(n_rep, -1, lanes)
    pieces = lax.all_to_all(packed, "rep", 0, 0, tiled=True)
    summed = pieces[0]
    for other in range(1, n_rep):
        summed = summed + pieces[other]
    summed = summed.reshape(-1)
    hidden_sum = summed[: probe_rows * 2 * rank_width].reshape(probe_rows, 2, rank_width)
    digest_sum = summed[probe_rows * 2 * rank_width :].reshape(blocks_all, 2, narrow)
    digest = 8.0 * digest_sum.transpose(1, 0, 2).reshape(2, blocks_all, 1, narrow)
    hidden = (jax.nn.silu(hidden_sum[:, 0]) * hidden_sum[:, 1]).astype(jnp.bfloat16)
    return (digest, hidden.reshape(1, 1, probe_rows, 1, rank_width))


def solution(mesh):
    n_fsdp = mesh.shape["fsdp"]
    n_ft = min(16, n_fsdp)
    devices = np.asarray(mesh.devices).reshape(
        n_ft, n_fsdp // n_ft, mesh.shape["rep"], mesh.shape["dp"]
    )
    split = Mesh(devices, ("ft", "fs", "rep", "dp"))
    placed = (P(FSDP, "dp", None), P(FSDP, "dp", None), P(), P(), P("rep", FSDP, None, None))
    return jax.shard_map(
        on_device,
        mesh=split,
        in_specs=placed,
        out_specs=(P(None, None, "dp", FSDP), P("rep", FSDP, None, "dp", None)),
        check_vma=False,
    )
```

```python
import jax
import jax.numpy as jnp
import numpy as np
from jax import lax
from jax.sharding import Mesh, PartitionSpec as P

FSDP = ("ft", "fs")


def on_device(trainer_gate, trainer_up, owner_map, sketch_seeds, probes):
    rows, _, width = trainer_gate.shape
    n_rep = lax.axis_size("rep")
    n_ft = lax.axis_size("ft")
    n_fs = lax.axis_size("fs")
    n_f = n_ft * n_fs
    total_rows = rows * n_f
    blocks_all = total_rows // 128
    rank_width = width // n_ft
    narrow = rank_width // n_fs
    quarter = 128 // n_rep
    piece = quarter // n_fs
    replica = lax.axis_index("rep")
    member = lax.axis_index("ft") * n_fs + lax.axis_index("fs")
    sub = lax.axis_index("fs")

    weights = jnp.stack([trainer_gate.reshape(rows, width), trainer_up.reshape(rows, width)])

    mine = lax.dynamic_slice_in_dim(weights, replica * quarter, quarter, 1)
    send = mine.reshape(2, n_fs, piece, n_ft, rank_width).transpose(3, 1, 2, 0, 4)
    send = send.reshape(n_ft, n_fs * piece, 2 * rank_width)

    positions = jnp.arange(blocks_all, dtype=jnp.int32)
    inverse = jnp.sum(
        jnp.where(owner_map[None, :] == positions[:, None], positions[None, :], 0), axis=1
    )

    probe_rows = probes.shape[2]
    wide = probes.reshape(probe_rows, total_rows).astype(jnp.float32)
    meansq = jnp.mean(wide * wide, axis=-1, keepdims=True)
    normed = (wide / jnp.sqrt(meansq + 1e-05)).astype(jnp.bfloat16)
    normed_send = normed.reshape(probe_rows, blocks_all, n_rep, quarter).transpose(2, 0, 1, 3)
    normed_send = normed_send.reshape(n_rep, probe_rows, blocks_all * quarter)

    signs = (1 - 2 * sketch_seeds).astype(jnp.float32).reshape(blocks_all, n_rep, quarter)
    own_signs = lax.dynamic_index_in_dim(signs, replica, 1, keepdims=False)
    sign_rows = jnp.eye(blocks_all, dtype=jnp.float32)[:, :, None] * own_signs[None, :, :]
    sign_rows = sign_rows.reshape(blocks_all, blocks_all * quarter).astype(jnp.bfloat16)

    send, normed_send = lax.optimization_barrier((send, normed_send))
    normed_recv = lax.all_to_all(normed_send, "rep", 0, 0, tiled=True)
    recv = lax.all_to_all(send, "ft", 0, 0, tiled=True)
    shared = [recv]
    for shift in range(1, n_fs):
        pairs = [(i, i ^ shift) for i in range(n_fs)]
        shared.append(lax.ppermute(recv, "fs", pairs))
    gathered = jnp.stack([shared[k] for k in range(n_fs)])
    source_of = sub ^ jnp.arange(n_fs, dtype=jnp.int32)
    gathered = gathered.reshape(n_fs, n_ft, quarter, 2 * rank_width)
    block_src = (jnp.arange(n_ft, dtype=jnp.int32)[None, :] * n_fs + source_of[:, None]).reshape(-1)
    gathered = gathered.reshape(n_fs * n_ft, quarter, 2 * rank_width)
    where_block = jnp.sum(
        jnp.where(block_src[None, :] == inverse[:, None], positions[None, :], 0), axis=1
    )
    ordered = jnp.take(gathered, where_block, axis=0)
    ordered = ordered.reshape(blocks_all * quarter, 2 * rank_width)

    lhs = jnp.concatenate(
        [normed_recv.reshape(n_rep * probe_rows, blocks_all * quarter), sign_rows], axis=0
    )
    partial = jnp.dot(lhs, ordered, preferred_element_type=jnp.float32)
    hidden_part = partial[: n_rep * probe_rows].reshape(n_rep, probe_rows * 2 * rank_width)
    digest_part = partial[n_rep * probe_rows :].reshape(blocks_all, 2, n_fs, narrow)
    digest_part = lax.dynamic_index_in_dim(digest_part, sub, 2, keepdims=False)
    digest_part = jnp.broadcast_to(digest_part.reshape(1, -1), (n_rep, blocks_all * 2 * narrow))
    lanes = 128
    packed = jnp.concatenate([hidden_part, digest_part], axis=1).reshape(n_rep, -1, lanes)
    pieces = lax.all_to_all(packed, "rep", 0, 0, tiled=True)
    summed = pieces[0]
    for other in range(1, n_rep):
        summed = summed + pieces[other]
    summed = summed.reshape(-1)
    hidden_sum = summed[: probe_rows * 2 * rank_width].reshape(probe_rows, 2, rank_width)
    digest_sum = summed[probe_rows * 2 * rank_width :].reshape(blocks_all, 2, narrow)
    digest = 8.0 * digest_sum.transpose(1, 0, 2).reshape(2, blocks_all, 1, narrow)
    hidden = (jax.nn.silu(hidden_sum[:, 0]) * hidden_sum[:, 1]).astype(jnp.bfloat16)
    return (digest, hidden.reshape(1, 1, probe_rows, 1, rank_width))


def solution(mesh):
    n_fsdp = mesh.shape["fsdp"]
    n_ft = min(16, n_fsdp)
    devices = np.asarray(mesh.devices).reshape(
        n_ft, n_fsdp // n_ft, mesh.shape["rep"], mesh.shape["dp"]
    )
    split = Mesh(devices, ("ft", "fs", "rep", "dp"))
    placed = (P(FSDP, "dp", None), P(FSDP, "dp", None), P(), P(), P("rep", FSDP, None, None))
    return jax.shard_map(
        on_device,
        mesh=split,
        in_specs=placed,
        out_specs=(P(None, None, "dp", FSDP), P("rep", FSDP, None, "dp", None)),
        check_vma=False,
    )
```

```python
import jax
import jax.numpy as jnp
import numpy as np
from jax import lax
from jax.sharding import Mesh, PartitionSpec as P

FSDP = ("ft", "fs")


def on_device(trainer_gate, trainer_up, owner_map, sketch_seeds, probes):
    rows, _, width = trainer_gate.shape
    n_rep = lax.axis_size("rep")
    n_ft = lax.axis_size("ft")
    n_fs = lax.axis_size("fs")
    n_f = n_ft * n_fs
    total_rows = rows * n_f
    blocks_all = total_rows // 128
    rank_width = width // n_ft
    narrow = rank_width // n_fs
    quarter = 128 // n_rep
    piece = quarter // n_fs
    replica = lax.axis_index("rep")
    member = lax.axis_index("ft") * n_fs + lax.axis_index("fs")
    sub = lax.axis_index("fs")

    weights = jnp.stack([trainer_gate.reshape(rows, width), trainer_up.reshape(rows, width)])

    mine = lax.dynamic_slice_in_dim(weights, replica * quarter, quarter, 1)
    send = mine.reshape(2, n_fs, piece, n_ft, rank_width).transpose(0, 3, 1, 2, 4)
    send = send.reshape(2, n_ft, n_fs * piece, rank_width)

    positions = jnp.arange(blocks_all, dtype=jnp.int32)
    inverse = jnp.sum(
        jnp.where(owner_map[None, :] == positions[:, None], positions[None, :], 0), axis=1
    )

    probe_rows = probes.shape[2]
    wide = probes.reshape(probe_rows, total_rows).astype(jnp.float32)
    meansq = jnp.mean(wide * wide, axis=-1, keepdims=True)
    normed = (wide / jnp.sqrt(meansq + 1e-05)).astype(jnp.bfloat16)
    normed_send = normed.reshape(probe_rows, blocks_all, n_rep, quarter).transpose(2, 0, 1, 3)
    normed_send = normed_send.reshape(n_rep, probe_rows, blocks_all * quarter)

    signs = (1 - 2 * sketch_seeds).astype(jnp.float32).reshape(blocks_all, n_rep, quarter)
    own_signs = lax.dynamic_index_in_dim(signs, replica, 1, keepdims=False)
    sign_rows = jnp.eye(blocks_all, dtype=jnp.float32)[:, :, None] * own_signs[None, :, :]
    sign_rows = sign_rows.reshape(blocks_all, blocks_all * quarter).astype(jnp.bfloat16)

    chunks = [
        lax.dynamic_index_in_dim(normed_send, (replica + k) % n_rep, 0, keepdims=False)
        for k in range(n_rep)
    ]
    chunks = list(lax.optimization_barrier((send, *chunks)))
    send, chunks = chunks[0], chunks[1:]
    normed_got = [chunks[0]]
    for k in range(1, n_rep):
        pairs = [(i, (i + k) % n_rep) for i in range(n_rep)]
        normed_got.append(lax.ppermute(chunks[k], "rep", pairs))
    source_of = sub ^ jnp.arange(n_fs, dtype=jnp.int32)
    block_src = (jnp.arange(n_ft, dtype=jnp.int32)[None, :] * n_fs + source_of[:, None]).reshape(-1)
    where_block = jnp.sum(
        jnp.where(block_src[None, :] == inverse[:, None], positions[None, :], 0), axis=1
    )
    lhs = jnp.concatenate([*normed_got, sign_rows], axis=0)

    partials = []
    for proj in range(2):
        recv = lax.all_to_all(send[proj], "ft", 0, 0, tiled=True)
        shared = [recv]
        for shift in range(1, n_fs):
            pairs = [(i, i ^ shift) for i in range(n_fs)]
            shared.append(lax.ppermute(recv, "fs", pairs))
        gathered = jnp.stack(shared).reshape(n_fs * n_ft, quarter, rank_width)
        ordered = jnp.take(gathered, where_block, axis=0)
        ordered = ordered.reshape(blocks_all * quarter, rank_width)
        partials.append(jnp.dot(lhs, ordered, preferred_element_type=jnp.float32))
    partial = jnp.concatenate(partials, axis=1)
    hidden_part = partial[: n_rep * probe_rows].reshape(n_rep, probe_rows * 2 * rank_width)
    digest_part = partial[n_rep * probe_rows :].reshape(blocks_all, 2, n_fs, narrow)
    digest_part = lax.dynamic_index_in_dim(digest_part, sub, 2, keepdims=False)
    digest_part = jnp.broadcast_to(digest_part.reshape(1, -1), (n_rep, blocks_all * 2 * narrow))
    lanes = 128
    packed = jnp.concatenate([hidden_part, digest_part], axis=1).reshape(n_rep, -1, lanes)
    back = [packed[0]]
    for k in range(1, n_rep):
        pairs = [(i, (i - k) % n_rep) for i in range(n_rep)]
        back.append(lax.ppermute(packed[k], "rep", pairs))
    slot_of = (jnp.arange(n_rep, dtype=jnp.int32) - replica) % n_rep
    pieces = jnp.take(jnp.stack(back), slot_of, axis=0)
    summed = pieces[0]
    for other in range(1, n_rep):
        summed = summed + pieces[other]
    summed = summed.reshape(-1)
    hidden_sum = summed[: probe_rows * 2 * rank_width].reshape(probe_rows, 2, rank_width)
    digest_sum = summed[probe_rows * 2 * rank_width :].reshape(blocks_all, 2, narrow)
    digest = 8.0 * digest_sum.transpose(1, 0, 2).reshape(2, blocks_all, 1, narrow)
    hidden = (jax.nn.silu(hidden_sum[:, 0]) * hidden_sum[:, 1]).astype(jnp.bfloat16)
    return (digest, hidden.reshape(1, 1, probe_rows, 1, rank_width))


def solution(mesh):
    n_fsdp = mesh.shape["fsdp"]
    n_ft = min(16, n_fsdp)
    devices = np.asarray(mesh.devices).reshape(
        n_ft, n_fsdp // n_ft, mesh.shape["rep"], mesh.shape["dp"]
    )
    split = Mesh(devices, ("ft", "fs", "rep", "dp"))
    placed = (P(FSDP, "dp", None), P(FSDP, "dp", None), P(), P(), P("rep", FSDP, None, None))
    return jax.shard_map(
        on_device,
        mesh=split,
        in_specs=placed,
        out_specs=(P(None, None, "dp", FSDP), P("rep", FSDP, None, "dp", None)),
        check_vma=False,
    )
```

```python
import jax
import jax.numpy as jnp
import numpy as np
from jax import lax
from jax.sharding import Mesh, PartitionSpec as P

FSDP = ("ft", "fs")


def on_device(trainer_gate, trainer_up, owner_map, sketch_seeds, probes):
    rows, _, width = trainer_gate.shape
    n_rep = lax.axis_size("rep")
    n_ft = lax.axis_size("ft")
    n_fs = lax.axis_size("fs")
    n_f = n_ft * n_fs
    total_rows = rows * n_f
    blocks_all = total_rows // 128
    rank_width = width // n_ft
    narrow = rank_width // n_fs
    quarter = 128 // n_rep
    piece = quarter // n_fs
    replica = lax.axis_index("rep")
    member = lax.axis_index("ft") * n_fs + lax.axis_index("fs")
    sub = lax.axis_index("fs")

    weights = jnp.stack([trainer_gate.reshape(rows, width), trainer_up.reshape(rows, width)])

    mine = lax.dynamic_slice_in_dim(weights, replica * quarter, quarter, 1)
    send = mine.reshape(2, n_fs, piece, n_ft, rank_width).transpose(3, 1, 2, 0, 4)
    send = send.reshape(n_ft, n_fs * piece, 2 * rank_width)

    positions = jnp.arange(blocks_all, dtype=jnp.int32)
    inverse = jnp.sum(
        jnp.where(owner_map[None, :] == positions[:, None], positions[None, :], 0), axis=1
    )

    probe_rows = probes.shape[2]
    wide = probes.reshape(probe_rows, total_rows).astype(jnp.float32)
    meansq = jnp.mean(wide * wide, axis=-1, keepdims=True)
    normed = (wide / jnp.sqrt(meansq + 1e-05)).astype(jnp.bfloat16)
    normed_send = normed.reshape(probe_rows, blocks_all, n_rep, quarter).transpose(2, 0, 1, 3)
    normed_send = normed_send.reshape(n_rep, probe_rows, blocks_all * quarter)

    signs = (1 - 2 * sketch_seeds).astype(jnp.float32).reshape(blocks_all, n_rep, quarter)
    own_signs = lax.dynamic_index_in_dim(signs, replica, 1, keepdims=False)
    sign_rows = jnp.eye(blocks_all, dtype=jnp.float32)[:, :, None] * own_signs[None, :, :]
    sign_rows = sign_rows.reshape(blocks_all, blocks_all * quarter).astype(jnp.bfloat16)

    chunks = [
        lax.dynamic_index_in_dim(normed_send, (replica + k) % n_rep, 0, keepdims=False)
        for k in range(n_rep)
    ]
    normed_got = [chunks[0]]
    for k in range(1, n_rep):
        pairs = [(i, (i + k) % n_rep) for i in range(n_rep)]
        normed_got.append(lax.ppermute(chunks[k], "rep", pairs))
    recv = lax.all_to_all(send, "ft", 0, 0, tiled=True)
    shared = [recv]
    for shift in range(1, n_fs):
        pairs = [(i, i ^ shift) for i in range(n_fs)]
        shared.append(lax.ppermute(recv, "fs", pairs))
    gathered = jnp.stack([shared[k] for k in range(n_fs)])
    source_of = sub ^ jnp.arange(n_fs, dtype=jnp.int32)
    gathered = gathered.reshape(n_fs, n_ft, quarter, 2 * rank_width)
    block_src = (jnp.arange(n_ft, dtype=jnp.int32)[None, :] * n_fs + source_of[:, None]).reshape(-1)
    gathered = gathered.reshape(n_fs * n_ft, quarter, 2 * rank_width)
    where_block = jnp.sum(
        jnp.where(block_src[None, :] == inverse[:, None], positions[None, :], 0), axis=1
    )
    ordered = jnp.take(gathered, where_block, axis=0)
    ordered = ordered.reshape(blocks_all * quarter, 2 * rank_width)

    lhs = jnp.concatenate(
        [*normed_got, sign_rows], axis=0
    )
    partial = jnp.dot(lhs, ordered, preferred_element_type=jnp.float32)
    hidden_part = partial[: n_rep * probe_rows].reshape(n_rep, probe_rows * 2 * rank_width)
    digest_part = partial[n_rep * probe_rows :].reshape(blocks_all, 2, n_fs, narrow)
    digest_part = lax.dynamic_index_in_dim(digest_part, sub, 2, keepdims=False)
    digest_part = jnp.broadcast_to(digest_part.reshape(1, -1), (n_rep, blocks_all * 2 * narrow))
    lanes = 128
    packed = jnp.concatenate([hidden_part, digest_part], axis=1).reshape(n_rep, -1, lanes)
    back = [packed[0]]
    for k in range(1, n_rep):
        pairs = [(i, (i - k) % n_rep) for i in range(n_rep)]
        back.append(lax.ppermute(packed[k], "rep", pairs))
    slot_of = (jnp.arange(n_rep, dtype=jnp.int32) - replica) % n_rep
    pieces = jnp.take(jnp.stack(back), slot_of, axis=0)
    summed = pieces[0]
    for other in range(1, n_rep):
        summed = summed + pieces[other]
    summed = summed.reshape(-1)
    hidden_sum = summed[: probe_rows * 2 * rank_width].reshape(probe_rows, 2, rank_width)
    digest_sum = summed[probe_rows * 2 * rank_width :].reshape(blocks_all, 2, narrow)
    digest = 8.0 * digest_sum.transpose(1, 0, 2).reshape(2, blocks_all, 1, narrow)
    hidden = (jax.nn.silu(hidden_sum[:, 0]) * hidden_sum[:, 1]).astype(jnp.bfloat16)
    return (digest, hidden.reshape(1, 1, probe_rows, 1, rank_width))


def solution(mesh):
    n_fsdp = mesh.shape["fsdp"]
    n_ft = min(16, n_fsdp)
    devices = np.asarray(mesh.devices).reshape(
        n_ft, n_fsdp // n_ft, mesh.shape["rep"], mesh.shape["dp"]
    )
    split = Mesh(devices, ("ft", "fs", "rep", "dp"))
    placed = (P(FSDP, "dp", None), P(FSDP, "dp", None), P(), P(), P("rep", FSDP, None, None))
    return jax.shard_map(
        on_device,
        mesh=split,
        in_specs=placed,
        out_specs=(P(None, None, "dp", FSDP), P("rep", FSDP, None, "dp", None)),
        check_vma=False,
    )
```

```python
import jax
import jax.numpy as jnp
import numpy as np
from jax import lax
from jax.sharding import Mesh, PartitionSpec as P

FSDP = ("ft", "fs")


def on_device(trainer_gate, trainer_up, owner_map, sketch_seeds, probes):
    rows, _, width = trainer_gate.shape
    n_rep = lax.axis_size("rep")
    n_ft = lax.axis_size("ft")
    n_fs = lax.axis_size("fs")
    n_f = n_ft * n_fs
    total_rows = rows * n_f
    blocks_all = total_rows // 128
    rank_width = width // n_ft
    narrow = rank_width // n_fs
    quarter = 128 // n_rep
    piece = quarter // n_fs
    replica = lax.axis_index("rep")
    member = lax.axis_index("ft") * n_fs + lax.axis_index("fs")
    sub = lax.axis_index("fs")

    weights = jnp.stack([trainer_gate.reshape(rows, width), trainer_up.reshape(rows, width)])

    mine = lax.dynamic_slice_in_dim(weights, replica * quarter, quarter, 1)
    send = mine.reshape(2, n_fs, piece, n_ft, rank_width).transpose(3, 1, 2, 0, 4)
    send = send.reshape(n_ft, n_fs * piece, 2 * rank_width)

    probe_rows = probes.shape[2]
    wide = probes.reshape(probe_rows, total_rows).astype(jnp.float32)
    meansq = jnp.mean(wide * wide, axis=-1, keepdims=True)
    normed = (wide / jnp.sqrt(meansq + 1e-05)).astype(jnp.bfloat16)
    normed_send = normed.reshape(probe_rows, blocks_all, n_rep, quarter).transpose(2, 0, 1, 3)
    normed_send = normed_send.reshape(n_rep, probe_rows, blocks_all * quarter)

    signs = (1 - 2 * sketch_seeds).astype(jnp.float32).reshape(blocks_all, n_rep, quarter)
    own_signs = lax.dynamic_index_in_dim(signs, replica, 1, keepdims=False)
    sign_rows = jnp.eye(blocks_all, dtype=jnp.float32)[:, :, None] * own_signs[None, :, :]
    sign_rows = sign_rows.reshape(blocks_all, blocks_all * quarter).astype(jnp.bfloat16)

    chunks = [
        lax.dynamic_index_in_dim(normed_send, (replica + k) % n_rep, 0, keepdims=False)
        for k in range(n_rep)
    ]
    normed_got = [chunks[0]]
    for k in range(1, n_rep):
        pairs = [(i, (i + k) % n_rep) for i in range(n_rep)]
        normed_got.append(lax.ppermute(chunks[k], "rep", pairs))
    recv = lax.all_to_all(send, "ft", 0, 0, tiled=True)
    shared = [recv]
    for shift in range(1, n_fs):
        pairs = [(i, i ^ shift) for i in range(n_fs)]
        shared.append(lax.ppermute(recv, "fs", pairs))
    source_of = sub ^ jnp.arange(n_fs, dtype=jnp.int32)
    block_src = (jnp.arange(n_ft, dtype=jnp.int32)[None, :] * n_fs + source_of[:, None]).reshape(-1)
    true_of_slot = owner_map[block_src]
    lhs = jnp.concatenate([*normed_got, sign_rows], axis=0)
    lhs_rows = lhs.shape[0]
    lhs = jnp.take(lhs.reshape(lhs_rows, blocks_all, quarter), true_of_slot, axis=1)
    lhs = lhs.reshape(lhs_rows, n_fs, n_ft * quarter)
    partial = None
    for k in range(n_fs):
        term = jnp.dot(
            lhs[:, k],
            shared[k].reshape(n_ft * quarter, 2 * rank_width),
            preferred_element_type=jnp.float32,
        )
        partial = term if partial is None else partial + term
    hidden_part = partial[: n_rep * probe_rows].reshape(n_rep, probe_rows * 2 * rank_width)
    digest_part = partial[n_rep * probe_rows :].reshape(blocks_all, 2, n_fs, narrow)
    digest_part = lax.dynamic_index_in_dim(digest_part, sub, 2, keepdims=False)
    digest_part = jnp.broadcast_to(digest_part.reshape(1, -1), (n_rep, blocks_all * 2 * narrow))
    lanes = 128
    packed = jnp.concatenate([hidden_part, digest_part], axis=1).reshape(n_rep, -1, lanes)
    back = [packed[0]]
    for k in range(1, n_rep):
        pairs = [(i, (i - k) % n_rep) for i in range(n_rep)]
        back.append(lax.ppermute(packed[k], "rep", pairs))
    slot_of = (jnp.arange(n_rep, dtype=jnp.int32) - replica) % n_rep
    pieces = jnp.take(jnp.stack(back), slot_of, axis=0)
    summed = pieces[0]
    for other in range(1, n_rep):
        summed = summed + pieces[other]
    summed = summed.reshape(-1)
    hidden_sum = summed[: probe_rows * 2 * rank_width].reshape(probe_rows, 2, rank_width)
    digest_sum = summed[probe_rows * 2 * rank_width :].reshape(blocks_all, 2, narrow)
    digest = 8.0 * digest_sum.transpose(1, 0, 2).reshape(2, blocks_all, 1, narrow)
    hidden = (jax.nn.silu(hidden_sum[:, 0]) * hidden_sum[:, 1]).astype(jnp.bfloat16)
    return (digest, hidden.reshape(1, 1, probe_rows, 1, rank_width))


def solution(mesh):
    n_fsdp = mesh.shape["fsdp"]
    n_ft = min(16, n_fsdp)
    devices = np.asarray(mesh.devices).reshape(
        n_ft, n_fsdp // n_ft, mesh.shape["rep"], mesh.shape["dp"]
    )
    split = Mesh(devices, ("ft", "fs", "rep", "dp"))
    placed = (P(FSDP, "dp", None), P(FSDP, "dp", None), P(), P(), P("rep", FSDP, None, None))
    return jax.shard_map(
        on_device,
        mesh=split,
        in_specs=placed,
        out_specs=(P(None, None, "dp", FSDP), P("rep", FSDP, None, "dp", None)),
        check_vma=False,
    )
```

```python
import jax
import jax.numpy as jnp
import numpy as np
from jax import lax
from jax.sharding import Mesh, PartitionSpec as P

FSDP = ("ft", "fs")


def on_device(trainer_gate, trainer_up, owner_map, sketch_seeds, probes):
    rows, _, width = trainer_gate.shape
    n_rep = lax.axis_size("rep")
    n_ft = lax.axis_size("ft")
    n_fs = lax.axis_size("fs")
    n_f = n_ft * n_fs
    total_rows = rows * n_f
    blocks_all = total_rows // 128
    rank_width = width // n_ft
    narrow = rank_width // n_fs
    quarter = 128 // n_rep
    piece = quarter // n_fs
    replica = lax.axis_index("rep")
    member = lax.axis_index("ft") * n_fs + lax.axis_index("fs")
    sub = lax.axis_index("fs")

    weights = jnp.stack([trainer_gate.reshape(rows, width), trainer_up.reshape(rows, width)])

    mine = lax.dynamic_slice_in_dim(weights, replica * quarter, quarter, 1)
    send = mine.reshape(2, n_fs, piece, n_ft, rank_width).transpose(3, 1, 2, 0, 4)
    send = send.reshape(n_ft, n_fs * piece, 2 * rank_width)

    probe_rows = probes.shape[2]
    wide = probes.reshape(probe_rows, total_rows).astype(jnp.float32)
    meansq = jnp.mean(wide * wide, axis=-1, keepdims=True)
    normed = (wide / jnp.sqrt(meansq + 1e-05)).astype(jnp.bfloat16)
    normed_send = normed.reshape(probe_rows, blocks_all, n_rep, quarter).transpose(2, 0, 1, 3)
    normed_send = normed_send.reshape(n_rep, probe_rows, blocks_all * quarter)

    signs = (1 - 2 * sketch_seeds).astype(jnp.float32).reshape(blocks_all, n_rep, quarter)
    own_signs = lax.dynamic_index_in_dim(signs, replica, 1, keepdims=False)
    sign_rows = jnp.eye(blocks_all, dtype=jnp.float32)[:, :, None] * own_signs[None, :, :]
    sign_rows = sign_rows.reshape(blocks_all, blocks_all * quarter).astype(jnp.bfloat16)

    chunks = [
        lax.dynamic_index_in_dim(normed_send, (replica + k) % n_rep, 0, keepdims=False)
        for k in range(n_rep)
    ]
    normed_got = [chunks[0]]
    for k in range(1, n_rep):
        pairs = [(i, (i + k) % n_rep) for i in range(n_rep)]
        normed_got.append(lax.ppermute(chunks[k], "rep", pairs))
    recv = lax.all_to_all(send, "ft", 0, 0, tiled=True)
    shared = [recv]
    for shift in range(1, n_fs):
        pairs = [(i, i ^ shift) for i in range(n_fs)]
        shared.append(lax.ppermute(recv, "fs", pairs))
    source_of = sub ^ jnp.arange(n_fs, dtype=jnp.int32)
    block_src = (jnp.arange(n_ft, dtype=jnp.int32)[None, :] * n_fs + source_of[:, None]).reshape(-1)
    true_of_slot = owner_map[block_src]
    lhs = jnp.concatenate([*normed_got, sign_rows], axis=0)
    lhs_rows = lhs.shape[0]
    lhs = jnp.take(lhs.reshape(lhs_rows, blocks_all, quarter), true_of_slot, axis=1)
    lhs = lhs.reshape(lhs_rows, n_fs, n_ft * quarter)
    partial = None
    for k in range(n_fs):
        term = jnp.dot(
            lhs[:, k],
            shared[k].reshape(n_ft * quarter, 2 * rank_width),
            preferred_element_type=jnp.float32,
        )
        partial = term if partial is None else partial + term
    width2 = 2 * rank_width
    hidden_part = partial[: n_rep * probe_rows].reshape(n_rep, probe_rows, width2)
    digest_part = partial[n_rep * probe_rows :].reshape(blocks_all, 2, n_fs, narrow)
    digest_part = lax.dynamic_index_in_dim(digest_part, sub, 2, keepdims=False)
    digest_rows = digest_part.reshape(-1, width2)
    back = []
    for k in range(n_rep):
        packed = jnp.concatenate([hidden_part[k], digest_rows], axis=0)
        if k > 0:
            pairs = [(i, (i - k) % n_rep) for i in range(n_rep)]
            packed = lax.ppermute(packed, "rep", pairs)
        back.append(packed)
    if n_rep == 4:
        summed = (back[0] + back[2]) + (back[1] + back[3])
    else:
        slot_of = (jnp.arange(n_rep, dtype=jnp.int32) - replica) % n_rep
        pieces = jnp.take(jnp.stack(back), slot_of, axis=0)
        summed = pieces[0]
        for other in range(1, n_rep):
            summed = summed + pieces[other]
    hidden_sum = summed[:probe_rows]
    digest_sum = summed[probe_rows:].reshape(blocks_all, 2, narrow)
    digest = 8.0 * digest_sum.transpose(1, 0, 2).reshape(2, blocks_all, 1, narrow)
    hidden = jax.nn.silu(hidden_sum[:, :rank_width]) * hidden_sum[:, rank_width:]
    hidden = hidden.astype(jnp.bfloat16)
    return (digest, hidden.reshape(1, 1, probe_rows, 1, rank_width))


def solution(mesh):
    n_fsdp = mesh.shape["fsdp"]
    n_ft = min(16, n_fsdp)
    devices = np.asarray(mesh.devices).reshape(
        n_ft, n_fsdp // n_ft, mesh.shape["rep"], mesh.shape["dp"]
    )
    split = Mesh(devices, ("ft", "fs", "rep", "dp"))
    placed = (P(FSDP, "dp", None), P(FSDP, "dp", None), P(), P(), P("rep", FSDP, None, None))
    return jax.shard_map(
        on_device,
        mesh=split,
        in_specs=placed,
        out_specs=(P(None, None, "dp", FSDP), P("rep", FSDP, None, "dp", None)),
        check_vma=False,
    )
```

```python
import jax
import jax.numpy as jnp
import numpy as np
from jax import lax
from jax.experimental import pallas as pl
from jax.experimental.pallas import tpu as pltpu
from jax.sharding import Mesh, PartitionSpec as P

FSDP = ("ft", "fs")


def combine_kernel(b0, b1, b2, b3, hidden_ref, digest_ref):
    rows, width = hidden_ref.shape
    total = (b0[...] + b2[...]) + (b1[...] + b3[...])
    gate = total[:rows, :width]
    up = total[:rows, width:]
    hidden_ref[...] = (gate / (1.0 + jnp.exp(-gate)) * up).astype(hidden_ref.dtype)
    digest_ref[...] = 8.0 * total[rows:, :]


def combine(back, probe_rows, rank_width):
    block_rows, width2 = back[0].shape
    vmem = pl.BlockSpec(memory_space=pltpu.VMEM)
    return pl.pallas_call(
        combine_kernel,
        out_shape=(
            jax.ShapeDtypeStruct((probe_rows, rank_width), jnp.bfloat16),
            jax.ShapeDtypeStruct((block_rows - probe_rows, width2), jnp.float32),
        ),
        in_specs=[vmem] * 4,
        out_specs=(vmem, vmem),
        cost_estimate=pl.CostEstimate(
            flops=4 * block_rows * width2,
            transcendentals=probe_rows * rank_width,
            bytes_accessed=4 * 4 * block_rows * width2,
        ),
    )(*back)


def on_device(trainer_gate, trainer_up, owner_map, sketch_seeds, probes):
    rows, _, width = trainer_gate.shape
    n_rep = lax.axis_size("rep")
    n_ft = lax.axis_size("ft")
    n_fs = lax.axis_size("fs")
    n_f = n_ft * n_fs
    total_rows = rows * n_f
    blocks_all = total_rows // 128
    rank_width = width // n_ft
    narrow = rank_width // n_fs
    quarter = 128 // n_rep
    piece = quarter // n_fs
    replica = lax.axis_index("rep")
    member = lax.axis_index("ft") * n_fs + lax.axis_index("fs")
    sub = lax.axis_index("fs")

    weights = jnp.stack([trainer_gate.reshape(rows, width), trainer_up.reshape(rows, width)])

    mine = lax.dynamic_slice_in_dim(weights, replica * quarter, quarter, 1)
    send = mine.reshape(2, n_fs, piece, n_ft, rank_width).transpose(3, 1, 2, 0, 4)
    send = send.reshape(n_ft, n_fs * piece, 2 * rank_width)

    probe_rows = probes.shape[2]
    wide = probes.reshape(probe_rows, total_rows).astype(jnp.float32)
    meansq = jnp.mean(wide * wide, axis=-1, keepdims=True)
    normed = (wide / jnp.sqrt(meansq + 1e-05)).astype(jnp.bfloat16)
    normed_send = normed.reshape(probe_rows, blocks_all, n_rep, quarter).transpose(2, 0, 1, 3)
    normed_send = normed_send.reshape(n_rep, probe_rows, blocks_all * quarter)

    signs = (1 - 2 * sketch_seeds).astype(jnp.float32).reshape(blocks_all, n_rep, quarter)
    own_signs = lax.dynamic_index_in_dim(signs, replica, 1, keepdims=False)
    sign_rows = jnp.eye(blocks_all, dtype=jnp.float32)[:, :, None] * own_signs[None, :, :]
    sign_rows = sign_rows.reshape(blocks_all, blocks_all * quarter).astype(jnp.bfloat16)

    chunks = [
        lax.dynamic_index_in_dim(normed_send, (replica + k) % n_rep, 0, keepdims=False)
        for k in range(n_rep)
    ]
    normed_got = [chunks[0]]
    for k in range(1, n_rep):
        pairs = [(i, (i + k) % n_rep) for i in range(n_rep)]
        normed_got.append(lax.ppermute(chunks[k], "rep", pairs))
    recv = lax.all_to_all(send, "ft", 0, 0, tiled=True)
    shared = [recv]
    for shift in range(1, n_fs):
        pairs = [(i, i ^ shift) for i in range(n_fs)]
        shared.append(lax.ppermute(recv, "fs", pairs))
    source_of = sub ^ jnp.arange(n_fs, dtype=jnp.int32)
    block_src = (jnp.arange(n_ft, dtype=jnp.int32)[None, :] * n_fs + source_of[:, None]).reshape(-1)
    true_of_slot = owner_map[block_src]
    lhs = jnp.concatenate([*normed_got, sign_rows], axis=0)
    lhs_rows = lhs.shape[0]
    lhs = jnp.take(lhs.reshape(lhs_rows, blocks_all, quarter), true_of_slot, axis=1)
    lhs = lhs.reshape(lhs_rows, n_fs, n_ft * quarter)
    partial = None
    for k in range(n_fs):
        term = jnp.dot(
            lhs[:, k],
            shared[k].reshape(n_ft * quarter, 2 * rank_width),
            preferred_element_type=jnp.float32,
        )
        partial = term if partial is None else partial + term
    width2 = 2 * rank_width
    hidden_part = partial[: n_rep * probe_rows].reshape(n_rep, probe_rows, width2)
    digest_part = partial[n_rep * probe_rows :].reshape(blocks_all, 2, n_fs, narrow)
    digest_part = lax.dynamic_index_in_dim(digest_part, sub, 2, keepdims=False)
    digest_rows = digest_part.reshape(-1, width2)
    back = []
    for k in range(n_rep):
        packed = jnp.concatenate([hidden_part[k], digest_rows], axis=0)
        if k > 0:
            pairs = [(i, (i - k) % n_rep) for i in range(n_rep)]
            packed = lax.ppermute(packed, "rep", pairs)
        back.append(packed)
    if n_rep == 4:
        hidden, digest_rows = combine(back, probe_rows, rank_width)
    else:
        slot_of = (jnp.arange(n_rep, dtype=jnp.int32) - replica) % n_rep
        pieces = jnp.take(jnp.stack(back), slot_of, axis=0)
        summed = pieces[0]
        for other in range(1, n_rep):
            summed = summed + pieces[other]
        hidden_sum = summed[:probe_rows]
        digest_rows = 8.0 * summed[probe_rows:]
        hidden = jax.nn.silu(hidden_sum[:, :rank_width]) * hidden_sum[:, rank_width:]
        hidden = hidden.astype(jnp.bfloat16)
    digest_sum = digest_rows.reshape(blocks_all, 2, narrow)
    digest = digest_sum.transpose(1, 0, 2).reshape(2, blocks_all, 1, narrow)
    return (digest, hidden.reshape(1, 1, probe_rows, 1, rank_width))


def solution(mesh):
    n_fsdp = mesh.shape["fsdp"]
    n_ft = min(16, n_fsdp)
    devices = np.asarray(mesh.devices).reshape(
        n_ft, n_fsdp // n_ft, mesh.shape["rep"], mesh.shape["dp"]
    )
    split = Mesh(devices, ("ft", "fs", "rep", "dp"))
    placed = (P(FSDP, "dp", None), P(FSDP, "dp", None), P(), P(), P("rep", FSDP, None, None))
    return jax.shard_map(
        on_device,
        mesh=split,
        in_specs=placed,
        out_specs=(P(None, None, "dp", FSDP), P("rep", FSDP, None, "dp", None)),
        check_vma=False,
    )
```

```python
import jax
import jax.numpy as jnp
import numpy as np
from jax import lax
from jax.sharding import Mesh, PartitionSpec as P

FSDP = ("ft", "fs")


def on_device(trainer_gate, trainer_up, owner_map, sketch_seeds, probes):
    rows, _, width = trainer_gate.shape
    n_rep = lax.axis_size("rep")
    n_ft = lax.axis_size("ft")
    n_fs = lax.axis_size("fs")
    n_f = n_ft * n_fs
    total_rows = rows * n_f
    blocks_all = total_rows // 128
    rank_width = width // n_ft
    narrow = rank_width // n_fs
    quarter = 128 // n_rep
    piece = quarter // n_fs
    replica = lax.axis_index("rep")
    member = lax.axis_index("ft") * n_fs + lax.axis_index("fs")
    sub = lax.axis_index("fs")

    weights = jnp.stack([trainer_gate.reshape(rows, width), trainer_up.reshape(rows, width)])

    mine = lax.dynamic_slice_in_dim(weights, replica * quarter, quarter, 1)
    send = mine.reshape(2, n_fs, piece, n_ft, rank_width).transpose(3, 0, 1, 2, 4)
    send = send.reshape(n_ft, 2 * quarter, rank_width)

    probe_rows = probes.shape[2]
    wide = probes.reshape(probe_rows, total_rows).astype(jnp.float32)
    meansq = jnp.mean(wide * wide, axis=-1, keepdims=True)
    normed = (wide / jnp.sqrt(meansq + 1e-05)).astype(jnp.bfloat16)
    normed_send = normed.reshape(probe_rows, blocks_all, n_rep, quarter).transpose(2, 0, 1, 3)
    normed_send = normed_send.reshape(n_rep, probe_rows, blocks_all * quarter)

    signs = (1 - 2 * sketch_seeds).astype(jnp.float32).reshape(blocks_all, n_rep, quarter)
    own_signs = lax.dynamic_index_in_dim(signs, replica, 1, keepdims=False)
    sign_rows = jnp.eye(blocks_all, dtype=jnp.float32)[:, :, None] * own_signs[None, :, :]
    sign_rows = sign_rows.reshape(blocks_all, blocks_all * quarter).astype(jnp.bfloat16)

    chunks = [
        lax.dynamic_index_in_dim(normed_send, (replica + k) % n_rep, 0, keepdims=False)
        for k in range(n_rep)
    ]
    normed_got = [chunks[0]]
    for k in range(1, n_rep):
        pairs = [(i, (i + k) % n_rep) for i in range(n_rep)]
        normed_got.append(lax.ppermute(chunks[k], "rep", pairs))
    recv = lax.all_to_all(send, "ft", 0, 0, tiled=True)
    shared = [recv]
    for shift in range(1, n_fs):
        pairs = [(i, i ^ shift) for i in range(n_fs)]
        shared.append(lax.ppermute(recv, "fs", pairs))
    source_of = sub ^ jnp.arange(n_fs, dtype=jnp.int32)
    block_src = (jnp.arange(n_ft, dtype=jnp.int32)[None, :] * n_fs + source_of[:, None]).reshape(-1)
    true_of_slot = owner_map[block_src]
    lhs = jnp.concatenate([*normed_got, sign_rows], axis=0)
    lhs_rows = lhs.shape[0]
    lhs = jnp.take(lhs.reshape(lhs_rows, blocks_all, quarter), true_of_slot, axis=1)
    lhs = lhs.reshape(lhs_rows, n_fs, n_ft * quarter)
    partial = None
    for k in range(n_fs):
        term = jnp.einsum(
            "mfq,fpqc->mpc",
            lhs[:, k].reshape(lhs_rows, n_ft, quarter),
            shared[k].reshape(n_ft, 2, quarter, rank_width),
            preferred_element_type=jnp.float32,
        ).reshape(lhs_rows, 2 * rank_width)
        partial = term if partial is None else partial + term
    width2 = 2 * rank_width
    hidden_part = partial[: n_rep * probe_rows].reshape(n_rep, probe_rows, width2)
    digest_part = partial[n_rep * probe_rows :].reshape(blocks_all, 2, n_fs, narrow)
    digest_part = lax.dynamic_index_in_dim(digest_part, sub, 2, keepdims=False)
    digest_rows = digest_part.reshape(-1, width2)
    back = []
    for k in range(n_rep):
        packed = jnp.concatenate([hidden_part[k], digest_rows], axis=0)
        if k > 0:
            pairs = [(i, (i - k) % n_rep) for i in range(n_rep)]
            packed = lax.ppermute(packed, "rep", pairs)
        back.append(packed)
    if n_rep == 4:
        summed = (back[0] + back[2]) + (back[1] + back[3])
    else:
        slot_of = (jnp.arange(n_rep, dtype=jnp.int32) - replica) % n_rep
        pieces = jnp.take(jnp.stack(back), slot_of, axis=0)
        summed = pieces[0]
        for other in range(1, n_rep):
            summed = summed + pieces[other]
    hidden_sum = summed[:probe_rows]
    digest_sum = summed[probe_rows:].reshape(blocks_all, 2, narrow)
    digest = 8.0 * digest_sum.transpose(1, 0, 2).reshape(2, blocks_all, 1, narrow)
    hidden = jax.nn.silu(hidden_sum[:, :rank_width]) * hidden_sum[:, rank_width:]
    hidden = hidden.astype(jnp.bfloat16)
    return (digest, hidden.reshape(1, 1, probe_rows, 1, rank_width))


def solution(mesh):
    n_fsdp = mesh.shape["fsdp"]
    n_ft = min(16, n_fsdp)
    devices = np.asarray(mesh.devices).reshape(
        n_ft, n_fsdp // n_ft, mesh.shape["rep"], mesh.shape["dp"]
    )
    split = Mesh(devices, ("ft", "fs", "rep", "dp"))
    placed = (P(FSDP, "dp", None), P(FSDP, "dp", None), P(), P(), P("rep", FSDP, None, None))
    return jax.shard_map(
        on_device,
        mesh=split,
        in_specs=placed,
        out_specs=(P(None, None, "dp", FSDP), P("rep", FSDP, None, "dp", None)),
        check_vma=False,
    )
```
